32 devices in a mesh: member: 8 (over z, x), space: 4 (over y, core).
Axes of the slice: x: 2, y: 2, z: 4, core: 2. Of those that a mesh axis runs over, the one named last changes fastest.
Arguments:
- alpha: float32 [16, 16, 32, 1280], P('member', None, 'space'), may hold values from -6 to 6
- perturb: bfloat16 [4, 16, 16, 32, 1280], P(None, 'member', None, 'space'), may hold values from -1.5 to 1.5
- kappa: float32 [32, 1280], P('space'), may hold values from 0.1 to 0.24
- land: int32 [32, 1280], P('space'), may hold values 0 or 1
- obs_weight: float32 [4, 16, 32, 1280], P(None, 'member', 'space'), may hold values from 0.2 to 5
- innovation: float32 [4, 16, 32, 1280], P(None, 'member', 'space'), may hold values from -6 to 6
Outputs:
- gradient: float32 [16, 16, 32, 1280], P('member', None, 'space')
- weighted_misfit: float32 [4, 16, 32, 1280], P(None, 'member', 'space')
The draws below stay inside these ranges and needn't reach their ends.
All inputs are finite; a program needn't handle non-finite values. No bound on the sum of `land` on one device may be relied on, other than what follows from the above.
Results may differ from the reference program's by a relative error of at most 0.0003.
Values sent between devices are 32-bit elements; how exact they have to be, the bound alone decides.
No kernel may reach another device: no remote copies, remote signals or barrier semaphores. Data moves between devices by JAX's collectives and lax.ppermute only.
A program may use at most 64 MiB of HBM per device.

```python
import math
import jax
import jax.numpy as jnp
from jax import lax

FIELDS = 2
LEVELS = 8
SLOTS = 4
STEPS = 4
LON = 1280
MEMBERS = 16
LAT = 32


def set_ends(array, stream_key, low, largest):
    shape = array.shape
    spot = [jax.random.randint(jax.random.fold_in(stream_key, axis), (), 0, shape[axis]) for axis in range(len(shape))]
    array = array.at[tuple(spot)].set(low)
    longest = shape.index(max(shape))
    spot[longest] = (spot[longest] + 1) % shape[longest]
    return array.at[tuple(spot)].set(largest)


def shard_levels(rng, shape, split, least, top_value):
    def one(position, shards_of):
        draws = jax.random.uniform(jax.random.fold_in(jax.random.fold_in(rng, 6), position), (shards_of,), jnp.float32, least / len(split), top_value / len(split))
        return jnp.repeat(jnp.exp(draws), shape[position] // shards_of).reshape((-1,) + (1,) * (len(shape) - position - 1))

    gain = one(*split[0])
    for cut in split[1:]:
        gain = gain * one(*cut)
    return gain


def noise(stream_key, extent, deviation, bound, split=(), kind=jnp.bfloat16):
    level = shard_levels(stream_key, extent, split, -0.22, 0.18) if split else 1.0
    values = jax.random.normal(stream_key, extent, jnp.float32) * deviation * level
    return jnp.minimum(jnp.maximum(values, -bound), bound).astype(kind)


def setup_inputs(seed: int = 0) -> dict:
    arg_keys = jax.random.split(jax.random.key(seed), 7)
    alpha = noise(arg_keys[0], (MEMBERS, FIELDS * LEVELS, LAT, LON), 1.0, 6.0, ((0, 8), (2, 4)), jnp.float32)
    perturb = noise(arg_keys[1], (SLOTS, MEMBERS, FIELDS * LEVELS, LAT, LON), MEMBERS ** -0.5, 1.5, ((1, 8), (3, 4)))
    kappa = jnp.clip(0.1 + 0.13999999 * jax.random.uniform(arg_keys[2], (LAT, LON), jnp.float32) ** shard_levels(arg_keys[2], (LAT, LON), ((0, 4),), -0.2, 0.2), 0.1, 0.24)
    land = set_ends((jax.random.randint(arg_keys[3], (LAT, LON), 0, 4) < 3).astype(jnp.int32), jax.random.fold_in(arg_keys[3], 1), 0, 1)
    obs_weight = jnp.clip(jnp.exp(math.log(5.0) - 3.218876 * jax.random.uniform(arg_keys[4], (SLOTS, FIELDS * LEVELS, LAT, LON), jnp.float32) ** shard_levels(arg_keys[4], (SLOTS, FIELDS * LEVELS, LAT, LON), ((1, 8), (2, 4)), -0.2, 0.2)), 0.2, 5.0)
    innovation = noise(arg_keys[5], (SLOTS, FIELDS * LEVELS, LAT, LON), 1.0, 6.0, ((1, 8), (2, 4)), jnp.float32)
    return {"alpha": alpha, "perturb": perturb, "kappa": kappa, "land": land, "obs_weight": obs_weight, "innovation": innovation}


def face_terms(kappa):
    padded = jnp.pad(kappa, ((1, 1), (0, 0)))
    coef_north = 0.5 * (padded[1:-1] + padded[2:])
    coef_south = 0.5 * (padded[1:-1] + padded[:-2])
    coef_east = 0.5 * (kappa + jnp.roll(kappa, -1, axis=1))
    coef_west = 0.5 * (kappa + jnp.roll(kappa, 1, axis=1))
    return coef_east, coef_west, coef_north, coef_south


def diffuse(field, faces):
    coef_east, coef_west, coef_north, coef_south = faces
    current = field
    for sweep in range(STEPS):
        padded = jnp.pad(current, ((0, 0), (1, 1), (0, 0)))
        current = (current + coef_east * (jnp.roll(current, -1, axis=-1) - current)
                   + coef_west * (jnp.roll(current, 1, axis=-1) - current)
                   + coef_north * (padded[:, 2:, :] - current)
                   + coef_south * (padded[:, :-2, :] - current))
    return current


def reference(alpha, perturb, kappa, land, obs_weight, innovation):
    faces = face_terms(kappa)
    sea = land.astype(jnp.float32)

    def forward(total, member):
        local = diffuse(alpha[member], faces) * sea
        return total + perturb[:, member].astype(jnp.float32) * local[None], None

    start = jnp.zeros(obs_weight.shape, jnp.float32)
    increment, unused = lax.scan(forward, start, jnp.arange(MEMBERS))
    weighted_misfit = obs_weight * (increment - innovation)

    def adjoint(member):
        back = jnp.sum(perturb[:, member].astype(jnp.float32) * weighted_misfit, axis=0)
        return diffuse(back * sea, faces) + alpha[member]

    gradient = lax.map(adjoint, jnp.arange(MEMBERS))
    return gradient, weighted_misfit
```

```python
import functools

import jax
import jax.numpy as jnp
from jax import lax
from jax.experimental import pallas as pl
from jax.experimental.pallas import tpu as pltpu
from jax.sharding import PartitionSpec as P

STEPS = 4
F32 = jnp.float32


def fill_faces(faces, kappa, above, below):
    width = kappa.shape[-1]
    beyond = jnp.concatenate([above, below], axis=0)
    row = lax.broadcasted_iota(jnp.int32, kappa.shape, 0)
    last = row == kappa.shape[0] - 1
    here, there = pltpu.roll(kappa, 7, 0), pltpu.roll(beyond, 7, 0)
    faces[0] = 0.5 * (kappa + pltpu.roll(kappa, width - 1, 1))
    faces[1] = 0.5 * (beyond + pltpu.roll(beyond, width - 1, 1))
    faces[2] = 0.5 * (kappa + jnp.where(last, there, here))
    faces[3] = 0.5 * (beyond + jnp.where(last, here, there))
    place, count = lax.axis_index("space"), lax.axis_size("space")
    has_above = (place < count - 1).astype(F32)
    has_below = (place > 0).astype(F32)
    faces[4] = jnp.where(row < 4, has_above, has_below)


def diffuse(faces, u, h):
    width = u.shape[-1]
    row = lax.broadcasted_iota(jnp.int32, u.shape, 0)
    last, first = row == u.shape[0] - 1, row == 0

    def along(v, face):
        flux = face * (pltpu.roll(v, width - 1, 1) - v)
        return flux - pltpu.roll(flux, 1, 1)

    for sweep in range(STEPS):
        ru, rh = pltpu.roll(u, 7, 0), pltpu.roll(h, 7, 0)
        fu = faces[2] * (jnp.where(last, rh, ru) - u)
        fh = faces[3] * (jnp.where(last, ru, rh) - h)
        su, sh = pltpu.roll(fu, 1, 0), pltpu.roll(fh, 1, 0)
        v = u + along(u, faces[0]) + (fu - jnp.where(first, sh, su))
        if sweep < STEPS - 1:
            h = faces[4] * (h + along(h, faces[1]) + (fh - jnp.where(first, su, sh)))
        u = v
    return u


def place_of(index, bits):
    owner = 0
    for k, bit in enumerate(reversed(bits)):
        owner = owner + ((index >> k) & 1) * bit
    return owner


def index_of(owner, bits):
    index = 0
    for bit in bits:
        index = index * 2 + jnp.where((owner & bit) != 0, 1, 0)
    return index


def forward_kernel(chunk, width, orders, alpha, above, below, k_above, k_below, kappa, land,
                   perturb, a_send, a_keep, b_send, b_keep, faces):
    slots, members = perturb.shape[:2]
    first_a, first_b = orders
    count = 2 * a_send.shape[0]
    me = lax.axis_index("member")
    fill_faces(faces, kappa[...], k_above[...], k_below[...])
    for half, out in ((1, a_send), (0, a_keep)):
        def level(i, carry, half=half, out=out):
            owner = place_of(i, first_a[1:]) + half * first_a[0]
            piece = owner ^ me
            row = piece * width + chunk
            local = []
            for m in range(members):
                h = jnp.concatenate([above[m * count + piece], below[m * count + piece]], axis=0)
                local.append(diffuse(faces, alpha[m, row], h) * land[...].astype(F32))
            def added(t):
                total = perturb[t, 0, row].astype(F32) * local[0]
                for m in range(1, members):
                    total = total + perturb[t, m, row].astype(F32) * local[m]
                return total
            for t in range(slots - 1):
                out[i, t] = added(t)
            tail = added(slots - 1)
            at = index_of(owner, first_b[1:])
            sends = (owner & first_b[0]) != 0

            @pl.when(sends)
            def _():
                b_send[at, 0] = tail

            @pl.when(jnp.logical_not(sends))
            def _():
                b_keep[at, 0] = tail
            return carry
        lax.fori_loop(0, count // 2, level, 0)


def back_kernel(chunk, width, orders, perturb, land, a_low, a_high, b_low, b_high,
                back, to_below, to_above):
    slots, members = perturb.shape[:2]
    first_a, first_b = orders
    count = 2 * a_low.shape[0]
    me = lax.axis_index("member")
    for half, given in ((0, a_low), (1, a_high)):
        def level(i, carry, half=half, given=given):
            owner = place_of(i, first_a[1:]) + half * first_a[0]
            piece = owner ^ me
            row = piece * width + chunk
            sea = land[...].astype(F32)
            at = index_of(owner, first_b[1:])
            tail = jnp.where((owner & first_b[0]) != 0, b_high[at, 0], b_low[at, 0])
            for m in range(members):
                total = perturb[slots - 1, m, row].astype(F32) * tail
                for t in range(slots - 1):
                    total = total + perturb[t, m, row].astype(F32) * given[i, t]
                total = total * sea
                back[m, piece] = total
                to_below[m * count + piece] = total[:4]
                to_above[m * count + piece] = total[4:]
            return carry
        lax.fori_loop(0, count // 2, level, 0)


def adjoint_kernel(chunk, width, alpha, back, above, below, k_above, k_below, kappa, gradient, faces):
    members, count = back.shape[:2]
    fill_faces(faces, kappa[...], k_above[...], k_below[...])

    def level(piece, carry):
        row = piece * width + chunk
        for m in range(members):
            h = jnp.concatenate([above[m * count + piece], below[m * count + piece]], axis=0)
            gradient[m, piece] = diffuse(faces, back[m, piece], h) + alpha[m, row]
        return carry
    lax.fori_loop(0, count, level, 0)


VMEM = pl.BlockSpec(memory_space=pltpu.VMEM)


def call(kernel, args, outs, scratch=()):
    return pl.pallas_call(
        kernel,
        out_shape=[jax.ShapeDtypeStruct(shape, F32) for shape in outs],
        in_specs=[VMEM] * len(args),
        out_specs=[VMEM] * len(outs),
        scratch_shapes=[pltpu.VMEM(shape, F32) for shape in scratch],
    )(*args)


def exchange(x, bit):
    count = lax.axis_size("member")
    return lax.ppermute(x, "member", [(i, i ^ bit) for i in range(count)])


def scatter(send, keep, bits):
    got = exchange(send, bits[0])
    for bit in bits[1:]:
        half = keep.shape[0] // 2
        send = keep[half:] + got[half:]
        keep = keep[:half] + got[:half]
        got = exchange(send, bit)
    return keep + got


def gather(own, bits):
    held = own
    for bit in reversed(bits[1:]):
        held = jnp.concatenate([held, exchange(held, bit)], axis=0)
    return held, exchange(held, bits[0])


def body(alpha, perturb, kappa, land, obs_weight, innovation):
    members, levels, rows, lon = alpha.shape
    slots = perturb.shape[0]
    count = lax.axis_size("member")
    width = obs_weight.shape[1]
    ends = lax.axis_size("space")
    up = [(i, i + 1) for i in range(ends - 1)]
    down = [(i + 1, i) for i in range(ends - 1)]
    bits = [1 << k for k in range(count.bit_length() - 1)]
    first_a, first_b = bits, [bits[1], bits[0]] + bits[2:]
    orders = (first_a, first_b)

    split = alpha.reshape(members, count, width, rows, lon)
    halos = []
    for c in range(width):
        mine = split[:, :, c].reshape(members * count, rows, lon)
        low, high = mine[:, :4], mine[:, 4:]
        if c == 0:
            low = jnp.concatenate([low, kappa[None, :4]], axis=0)
            high = jnp.concatenate([high, kappa[None, 4:]], axis=0)
        halos.append((lax.ppermute(low, "space", down), lax.ppermute(high, "space", up)))
    k_above, k_below = halos[0][0][-1], halos[0][1][-1]

    misfits = []
    parts = []
    for c in range(width):
        half = (count // 2,)
        a_send, a_keep, b_send, b_keep = call(
            functools.partial(forward_kernel, c, width, orders),
            (alpha, *halos[c], k_above, k_below, kappa, land, perturb),
            [half + (slots - 1, rows, lon)] * 2 + [half + (1, rows, lon)] * 2,
            [(5, rows, lon)],
        )
        own_a = scatter(a_send, a_keep, first_a)[0]
        own_b = scatter(b_send, b_keep, first_b)[0]
        misfit_a = obs_weight[: slots - 1, c] * (own_a - innovation[: slots - 1, c])
        misfit_b = obs_weight[slots - 1 :, c] * (own_b - innovation[slots - 1 :, c])
        misfits.append(jnp.concatenate([misfit_a, misfit_b], axis=0))
        parts.append(gather(misfit_a[None], first_a) + gather(misfit_b[None], first_b))

    backs = []
    for c in range(width):
        back, to_below, to_above = call(
            functools.partial(back_kernel, c, width, orders),
            (perturb, land, *parts[c]),
            [(members, count, rows, lon)] + [(members * count, 4, lon)] * 2,
        )
        backs.append((back, lax.ppermute(to_below, "space", down), lax.ppermute(to_above, "space", up)))
    gradients = []
    for c in range(width):
        back, above, below = backs[c]
        (gradient,) = call(
            functools.partial(adjoint_kernel, c, width),
            (alpha, back, above, below, k_above, k_below, kappa),
            [(members, count, rows, lon)],
            [(5, rows, lon)],
        )
        gradients.append(gradient)
    gradient = jnp.stack(gradients, axis=2).reshape(alpha.shape)
    return gradient, jnp.stack(misfits, axis=1)


def solution(mesh):
    placed = (
        P("member", None, "space", None),
        P(None, "member", None, "space", None),
        P("space", None),
        P("space", None),
        P(None, "member", "space", None),
        P(None, "member", "space", None),
    )
    return jax.shard_map(
        body,
        mesh=mesh,
        in_specs=placed,
        out_specs=(P("member", None, "space", None), P(None, "member", "space", None)),
        check_vma=False,
    )
```

```python
import functools

import jax
import jax.numpy as jnp
from jax import lax
from jax.experimental import pallas as pl
from jax.experimental.pallas import tpu as pltpu
from jax.sharding import PartitionSpec as P

STEPS = 4
F32 = jnp.float32


def fill_faces(faces, kappa, above, below):
    width = kappa.shape[-1]
    beyond = jnp.concatenate([above, below], axis=0)
    row = lax.broadcasted_iota(jnp.int32, kappa.shape, 0)
    last = row == kappa.shape[0] - 1
    here, there = pltpu.roll(kappa, 7, 0), pltpu.roll(beyond, 7, 0)
    faces[0] = 0.5 * (kappa + pltpu.roll(kappa, width - 1, 1))
    faces[1] = 0.5 * (beyond + pltpu.roll(beyond, width - 1, 1))
    faces[2] = 0.5 * (kappa + jnp.where(last, there, here))
    faces[3] = 0.5 * (beyond + jnp.where(last, here, there))
    place, count = lax.axis_index("space"), lax.axis_size("space")
    has_above = (place < count - 1).astype(F32)
    has_below = (place > 0).astype(F32)
    faces[4] = jnp.where(row < 4, has_above, has_below)


def diffuse(faces, u, h):
    width = u.shape[-1]
    row = lax.broadcasted_iota(jnp.int32, u.shape, 0)
    last, first = row == u.shape[0] - 1, row == 0

    def along(v, face):
        flux = face * (pltpu.roll(v, width - 1, 1) - v)
        return flux - pltpu.roll(flux, 1, 1)

    for sweep in range(STEPS):
        ru, rh = pltpu.roll(u, 7, 0), pltpu.roll(h, 7, 0)
        fu = faces[2] * (jnp.where(last, rh, ru) - u)
        fh = faces[3] * (jnp.where(last, ru, rh) - h)
        su, sh = pltpu.roll(fu, 1, 0), pltpu.roll(fh, 1, 0)
        v = u + along(u, faces[0]) + (fu - jnp.where(first, sh, su))
        if sweep < STEPS - 1:
            h = faces[4] * (h + along(h, faces[1]) + (fh - jnp.where(first, su, sh)))
        u = v
    return u


def place_of(index, bits):
    owner = 0
    for k, bit in enumerate(reversed(bits)):
        owner = owner + ((index >> k) & 1) * bit
    return owner


def index_of(owner, bits):
    index = 0
    for bit in bits:
        index = index * 2 + jnp.where((owner & bit) != 0, 1, 0)
    return index


def forward_kernel(chunk, width, orders, alpha, above, below, k_above, k_below, kappa, land,
                   perturb, a_send, a_keep, b_send, b_keep, faces):
    slots, members = perturb.shape[:2]
    first_a, first_b = orders
    count = 2 * a_send.shape[0]
    me = lax.axis_index("member")
    fill_faces(faces, kappa[...], k_above[...], k_below[...])
    for half, out in ((1, a_send), (0, a_keep)):
        def level(i, carry, half=half, out=out):
            owner = place_of(i, first_a[1:]) + half * first_a[0]
            piece = owner ^ me
            row = piece * width + chunk
            local = []
            for m in range(members):
                h = jnp.concatenate([above[m * count + piece], below[m * count + piece]], axis=0)
                local.append(diffuse(faces, alpha[m, row], h) * land[...].astype(F32))
            def added(t):
                total = perturb[t, 0, row].astype(F32) * local[0]
                for m in range(1, members):
                    total = total + perturb[t, m, row].astype(F32) * local[m]
                return total
            for t in range(slots - 1):
                out[i, t] = added(t)
            tail = added(slots - 1)
            at = index_of(owner, first_b[1:])
            sends = (owner & first_b[0]) != 0

            @pl.when(sends)
            def _():
                b_send[at, 0] = tail

            @pl.when(jnp.logical_not(sends))
            def _():
                b_keep[at, 0] = tail
            return carry
        lax.fori_loop(0, count // 2, level, 0)


def back_kernel(chunk, width, orders, perturb, land, a_low, a_high, b_low, b_high,
                back, to_below, to_above):
    slots, members = perturb.shape[:2]
    first_a, first_b = orders
    count = 2 * a_low.shape[0]
    me = lax.axis_index("member")
    for half, given in ((0, a_low), (1, a_high)):
        def level(i, carry, half=half, given=given):
            owner = place_of(i, first_a[1:]) + half * first_a[0]
            piece = owner ^ me
            row = piece * width + chunk
            sea = land[...].astype(F32)
            at = index_of(owner, first_b[1:])
            tail = jnp.where((owner & first_b[0]) != 0, b_high[at, 0], b_low[at, 0])
            for m in range(members):
                total = perturb[slots - 1, m, row].astype(F32) * tail
                for t in range(slots - 1):
                    total = total + perturb[t, m, row].astype(F32) * given[i, t]
                total = total * sea
                back[m, piece] = total
                to_below[m * count + piece] = total[:4]
                to_above[m * count + piece] = total[4:]
            return carry
        lax.fori_loop(0, count // 2, level, 0)


def adjoint_kernel(chunk, width, alpha, back, above, below, k_above, k_below, kappa, gradient, faces):
    members, count = back.shape[:2]
    fill_faces(faces, kappa[...], k_above[...], k_below[...])

    def level(piece, carry):
        row = piece * width + chunk
        for m in range(members):
            h = jnp.concatenate([above[m * count + piece], below[m * count + piece]], axis=0)
            gradient[m, piece] = diffuse(faces, back[m, piece], h) + alpha[m, row]
        return carry
    lax.fori_loop(0, count, level, 0)


VMEM = pl.BlockSpec(memory_space=pltpu.VMEM)


def call(kernel, args, outs, scratch=()):
    return pl.pallas_call(
        kernel,
        out_shape=[jax.ShapeDtypeStruct(shape, F32) for shape in outs],
        in_specs=[VMEM] * len(args),
        out_specs=[VMEM] * len(outs),
        scratch_shapes=[pltpu.VMEM(shape, F32) for shape in scratch],
        compiler_params=pltpu.CompilerParams(vmem_limit_bytes=24 << 20),
    )(*args)


def exchange(x, bit):
    count = lax.axis_size("member")
    return lax.ppermute(x, "member", [(i, i ^ bit) for i in range(count)])


def scatter(send, keep, bits):
    got = exchange(send, bits[0])
    for bit in bits[1:]:
        half = keep.shape[0] // 2
        send = keep[half:] + got[half:]
        keep = keep[:half] + got[:half]
        got = exchange(send, bit)
    return keep + got


def gather(own, bits):
    held = own
    for bit in reversed(bits[1:]):
        held = jnp.concatenate([held, exchange(held, bit)], axis=0)
    return held, exchange(held, bits[0])


def body(alpha, perturb, kappa, land, obs_weight, innovation):
    members, levels, rows, lon = alpha.shape
    slots = perturb.shape[0]
    count = lax.axis_size("member")
    width = obs_weight.shape[1]
    ends = lax.axis_size("space")
    up = [(i, i + 1) for i in range(ends - 1)]
    down = [(i + 1, i) for i in range(ends - 1)]
    bits = [1 << k for k in range(count.bit_length() - 1)]
    first_a, first_b = bits, [bits[1], bits[0]] + bits[2:]
    orders = (first_a, first_b)

    split = alpha.reshape(members, count, width, rows, lon)
    halos = []
    for c in range(width):
        mine = split[:, :, c].reshape(members * count, rows, lon)
        low, high = mine[:, :4], mine[:, 4:]
        if c == 0:
            low = jnp.concatenate([low, kappa[None, :4]], axis=0)
            high = jnp.concatenate([high, kappa[None, 4:]], axis=0)
        halos.append((lax.ppermute(low, "space", down), lax.ppermute(high, "space", up)))
    k_above, k_below = halos[0][0][-1], halos[0][1][-1]

    misfits = []
    parts = []
    for c in range(width):
        half = (count // 2,)
        a_send, a_keep, b_send, b_keep = call(
            functools.partial(forward_kernel, c, width, orders),
            (alpha, *halos[c], k_above, k_below, kappa, land, perturb),
            [half + (slots - 1, rows, lon)] * 2 + [half + (1, rows, lon)] * 2,
            [(5, rows, lon)],
        )
        own_a = scatter(a_send, a_keep, first_a)[0]
        own_b = scatter(b_send, b_keep, first_b)[0]
        misfit_a = obs_weight[: slots - 1, c] * (own_a - innovation[: slots - 1, c])
        misfit_b = obs_weight[slots - 1 :, c] * (own_b - innovation[slots - 1 :, c])
        misfits.append(jnp.concatenate([misfit_a, misfit_b], axis=0))
        parts.append(gather(misfit_a[None], first_a) + gather(misfit_b[None], first_b))

    backs = []
    for c in range(width):
        back, to_below, to_above = call(
            functools.partial(back_kernel, c, width, orders),
            (perturb, land, *parts[c]),
            [(members, count, rows, lon)] + [(members * count, 4, lon)] * 2,
        )
        backs.append((back, lax.ppermute(to_below, "space", down), lax.ppermute(to_above, "space", up)))
    gradients = []
    for c in range(width):
        back, above, below = backs[c]
        (gradient,) = call(
            functools.partial(adjoint_kernel, c, width),
            (alpha, back, above, below, k_above, k_below, kappa),
            [(members, count, rows, lon)],
            [(5, rows, lon)],
        )
        gradients.append(gradient)
    gradient = jnp.stack(gradients, axis=2).reshape(alpha.shape)
    return gradient, jnp.stack(misfits, axis=1)


def solution(mesh):
    placed = (
        P("member", None, "space", None),
        P(None, "member", None, "space", None),
        P("space", None),
        P("space", None),
        P(None, "member", "space", None),
        P(None, "member", "space", None),
    )
    return jax.shard_map(
        body,
        mesh=mesh,
        in_specs=placed,
        out_specs=(P("member", None, "space", None), P(None, "member", "space", None)),
        check_vma=False,
    )
```

```python
import functools

import jax
import jax.numpy as jnp
from jax import lax
from jax.experimental import pallas as pl
from jax.experimental.pallas import tpu as pltpu
from jax.sharding import PartitionSpec as P


STEPS = 4
F32 = jnp.float32


def fill_faces(faces, kappa, beyond):
    width = kappa.shape[-1]
    row = lax.broadcasted_iota(jnp.int32, kappa.shape, 0)
    last = row == kappa.shape[0] - 1
    here, there = pltpu.roll(kappa, 7, 0), pltpu.roll(beyond, 7, 0)
    faces[0] = 0.5 * (kappa + pltpu.roll(kappa, width - 1, 1))
    faces[1] = 0.5 * (beyond + pltpu.roll(beyond, width - 1, 1))
    faces[2] = 0.5 * (kappa + jnp.where(last, there, here))
    faces[3] = 0.5 * (beyond + jnp.where(last, here, there))
    place, count = lax.axis_index("space"), lax.axis_size("space")
    has_above = (place < count - 1).astype(F32)
    has_below = (place > 0).astype(F32)
    faces[4] = jnp.where(row < 4, has_above, has_below)


def diffuse(faces, u, h):
    width = u.shape[-1]
    row = lax.broadcasted_iota(jnp.int32, u.shape, 0)
    last, first = row == u.shape[0] - 1, row == 0

    def along(v, face):
        flux = face * (pltpu.roll(v, width - 1, 1) - v)
        return flux - pltpu.roll(flux, 1, 1)

    for sweep in range(STEPS):
        ru, rh = pltpu.roll(u, 7, 0), pltpu.roll(h, 7, 0)
        fu = faces[2] * (jnp.where(last, rh, ru) - u)
        fh = faces[3] * (jnp.where(last, ru, rh) - h)
        su, sh = pltpu.roll(fu, 1, 0), pltpu.roll(fh, 1, 0)
        v = u + along(u, faces[0]) + (fu - jnp.where(first, sh, su))
        if sweep < STEPS - 1:
            h = faces[4] * (h + along(h, faces[1]) + (fh - jnp.where(first, su, sh)))
        u = v
    return u


def place_of(index, bits):
    owner = 0
    for k, bit in enumerate(reversed(bits)):
        owner = owner + ((index >> k) & 1) * bit
    return owner


def index_of(owner, bits):
    index = 0
    for bit in bits:
        index = index * 2 + jnp.where((owner & bit) != 0, 1, 0)
    return index


def forward_kernel(chunk, width, groups, alpha, beyond, k_beyond, kappa, land, perturb, *refs):
    faces, outs = refs[-1], refs[:-1]
    members = perturb.shape[1]
    count = 2 * outs[0].shape[0]
    me = lax.axis_index("member")
    fill_faces(faces, kappa[...], k_beyond[...])
    lead = groups[0][1]
    for half in (1, 0):
        def level(i, carry, half=half):
            owner = place_of(i, lead[1:]) + half * lead[0]
            piece = owner ^ me
            row = piece * width + chunk
            local = []
            for m in range(members):
                local.append(diffuse(faces, alpha[m, row], beyond[m * count + piece]) * land[...].astype(F32))

            def added(t):
                total = perturb[t, 0, row].astype(F32) * local[0]
                for m in range(1, members):
                    total = total + perturb[t, m, row].astype(F32) * local[m]
                return total

            for g, (slots, order) in enumerate(groups):
                send, keep = outs[2 * g : 2 * g + 2]
                if order == lead:
                    for k, t in enumerate(slots):
                        (send if half else keep)[i, k] = added(t)
                else:
                    at = index_of(owner, order[1:])
                    sends = (owner & order[0]) != 0
                    values = [added(t) for t in slots]

                    @pl.when(sends)
                    def _(values=values, send=send, at=at):
                        for k, value in enumerate(values):
                            send[at, k] = value

                    @pl.when(jnp.logical_not(sends))
                    def _(values=values, keep=keep, at=at):
                        for k, value in enumerate(values):
                            keep[at, k] = value
            return carry

        lax.fori_loop(0, count // 2, level, 0)


def back_kernel(chunk, width, groups, perturb, land, *refs):
    back, to_partner, to_next = refs[-3:]
    given = refs[:-3]
    members = perturb.shape[1]
    count = 2 * given[0].shape[0]
    me = lax.axis_index("member")
    even = lax.rem(lax.axis_index("space"), 2) == 0
    lead = groups[0][1]
    for half in (0, 1):
        def level(i, carry, half=half):
            owner = place_of(i, lead[1:]) + half * lead[0]
            piece = owner ^ me
            row = piece * width + chunk
            sea = land[...].astype(F32)
            totals = [None] * members
            for g, (slots, order) in enumerate(groups):
                low, high = given[2 * g : 2 * g + 2]
                for k, t in enumerate(slots):
                    if order == lead:
                        value = (high if half else low)[i, k]
                    else:
                        at = index_of(owner, order[1:])
                        value = jnp.where((owner & order[0]) != 0, high[at, k], low[at, k])
                    for m in range(members):
                        term = perturb[t, m, row].astype(F32) * value
                        totals[m] = term if totals[m] is None else totals[m] + term
            for m in range(members):
                total = totals[m] * sea
                back[m, piece] = total
                to_partner[m * count + piece] = jnp.where(even, total[4:], total[:4])
                to_next[m * count + piece] = jnp.where(even, total[:4], total[4:])
            return carry

        lax.fori_loop(0, count // 2, level, 0)


def adjoint_kernel(chunk, width, alpha, back, beyond, k_beyond, kappa, *refs):
    gradient, faces, stage, done = refs[-4:]
    members, count = back.shape[:2]
    fill_faces(faces, kappa[...], k_beyond[...])

    def copy(m, piece):
        return pltpu.make_async_copy(
            stage.at[m, piece], gradient.at[m, piece * width + chunk], done.at[m, piece]
        )

    def level(piece, carry):
        for m in range(members):
            value = diffuse(faces, back[m, piece], beyond[m * count + piece])
            stage[m, piece] = value + alpha[m, piece * width + chunk]
            copy(m, piece).start()
        return carry

    def finish(piece, carry):
        for m in range(members):
            copy(m, piece).wait()
        return carry

    lax.fori_loop(0, count, level, 0)
    lax.fori_loop(0, count, finish, 0)


VMEM = pl.BlockSpec(memory_space=pltpu.VMEM)
GRANT = pltpu.CompilerParams(vmem_limit_bytes=24 << 20)


def call(kernel, args, outs, scratch=()):
    return pl.pallas_call(
        kernel,
        out_shape=[jax.ShapeDtypeStruct(shape, F32) for shape in outs],
        in_specs=[VMEM] * len(args),
        out_specs=[VMEM] * len(outs),
        scratch_shapes=[pltpu.VMEM(shape, F32) for shape in scratch],
        compiler_params=GRANT,
    )(*args)


def exchange(x, bit):
    count = lax.axis_size("member")
    return lax.ppermute(x, "member", [(i, i ^ bit) for i in range(count)])


def halves(to_partner, to_next):
    ends = lax.axis_size("space")
    pairs = [(i, i ^ 1) for i in range(ends)]
    nexts = [(i, i + 1 if i % 2 else i - 1) for i in range(1, ends - 1)]
    near = lax.ppermute(to_partner, "space", pairs)
    far = lax.ppermute(to_next, "space", nexts)
    even = lax.rem(lax.axis_index("space"), 2) == 0
    return jnp.concatenate([jnp.where(even, near, far), jnp.where(even, far, near)], axis=1)


def scatter(send, keep, bits):
    got = exchange(send, bits[0])
    for bit in bits[1:-1]:
        half = keep.shape[0] // 2
        send = keep[half:] + got[half:]
        keep = keep[:half] + got[:half]
        got = exchange(send, bit)
    return keep, got


def gather(held, bits):
    for k in range(len(bits) - 2, 0, -1):
        got = exchange(held, bits[k])
        held = jnp.concatenate([held, got], axis=0)
    return held, exchange(held, bits[0])


def inner(alpha, perturb, kappa, land, obs_weight, innovation):
    members, _, rows, lon = alpha.shape
    slots = perturb.shape[0]
    count = lax.axis_size("member")
    width = obs_weight.shape[1]
    bits = [1 << k for k in range(count.bit_length() - 1)]
    early, late = tuple(range(slots // 2)), tuple(range(slots // 2, slots))
    plans = [((early, bits), (late, bits)) for _ in range(width)]

    even = lax.rem(lax.axis_index("space"), 2) == 0
    split = alpha.reshape(members, count, width, rows, lon)
    beyond = []
    for c in range(width):
        mine = split[:, :, c].reshape(members * count, rows, lon)
        if c == 0:
            mine = jnp.concatenate([mine, kappa[None]], axis=0)
        low, high = mine[:, :4], mine[:, 4:]
        beyond.append(halves(jnp.where(even, high, low), jnp.where(even, low, high)))
    k_beyond = beyond[0][-1]

    far_weight = exchange(obs_weight, bits[-1])
    apart = {}
    for c in range(width):
        for g, (group, order) in enumerate(plans[c]):
            span = slice(group[0], group[-1] + 1)
            apart[c, g] = (innovation[span, c], jnp.stack([obs_weight[span, c], far_weight[span, c]]))
    apart = lax.optimization_barrier(apart)

    misfits = [[] for _ in range(width)]
    parts = [[] for _ in range(width)]
    for c in range(width):
        half = (count // 2,)
        shapes = [half + (len(group), rows, lon) for group, order in plans[c] for _ in range(2)]
        sums = call(
            functools.partial(forward_kernel, c, width, plans[c]),
            (alpha, beyond[c], k_beyond, kappa, land, perturb),
            shapes,
            [(5, rows, lon)],
        )
        for g, (group, order) in enumerate(plans[c]):
            offset, weights = apart[c, g]
            keep, got = scatter(sums[2 * g], sums[2 * g + 1], order)
            both = keep + got
            both = jnp.stack([both[0] - offset, both[1]])
            got = exchange(both, bits[-1])
            misfit = weights * (both + got[::-1])
            misfits[c].append(misfit[0])
            parts[c].extend(gather(misfit, order))

    gradient = None
    for c in range(width):
        back, to_partner, to_next = call(
            functools.partial(back_kernel, c, width, plans[c]),
            (perturb, land, *parts[c]),
            [(members, count, rows, lon)] + [(members * count, 4, lon)] * 2,
        )
        args = [alpha, back, halves(to_partner, to_next), k_beyond, kappa]
        specs = [VMEM] * len(args)
        if gradient is not None:
            args.append(gradient)
            specs.append(pl.BlockSpec(memory_space=pl.ANY))
        gradient = pl.pallas_call(
            functools.partial(adjoint_kernel, c, width),
            out_shape=jax.ShapeDtypeStruct(alpha.shape, F32),
            in_specs=specs,
            out_specs=pl.BlockSpec(memory_space=pl.ANY),
            scratch_shapes=[
                pltpu.VMEM((5, rows, lon), F32),
                pltpu.VMEM((members, count, rows, lon), F32),
                pltpu.SemaphoreType.DMA((members, count)),
            ],
            input_output_aliases={5: 0} if c else {},
            compiler_params=GRANT,
        )(*args)
    misfit = jnp.stack([jnp.concatenate(m, axis=0) for m in misfits], axis=1)
    return gradient, misfit


def solution(mesh):
    placed = (
        P("member", None, "space", None),
        P(None, "member", None, "space", None),
        P("space", None),
        P("space", None),
        P(None, "member", "space", None),
        P(None, "member", "space", None),
    )
    return jax.shard_map(
        inner,
        mesh=mesh,
        in_specs=placed,
        out_specs=(P("member", None, "space", None), P(None, "member", "space", None)),
        check_vma=False,
    )
```

```python
import functools

import jax
import jax.numpy as jnp
from jax import lax
from jax.experimental import pallas as pl
from jax.experimental.pallas import tpu as pltpu
from jax.sharding import PartitionSpec as P


STEPS = 4
F32 = jnp.float32


OWN, BEYOND = pl.ds(0, 8), pl.ds(8, 8)
EVEN, ODD = pl.ds(0, 8, stride=2), pl.ds(1, 8, stride=2)
LANES = 128


def put(pair, rows, value):
    for j in range(pair.shape[0]):
        pair[j, rows, :] = value[:, j * LANES : (j + 1) * LANES]


def get(pair, rows):
    return jnp.concatenate([pair[j, rows, :] for j in range(pair.shape[0])], axis=1)


def fill_faces(faces, pair, kappa, beyond):
    width = kappa.shape[-1]
    put(pair, OWN, kappa)
    put(pair, BEYOND, beyond)
    even, odd = get(pair, EVEN), get(pair, ODD)
    row = lax.broadcasted_iota(jnp.int32, kappa.shape, 0)
    place, count = lax.axis_index("space"), lax.axis_size("space")
    has_above = (place < count - 1).astype(F32)
    has_below = (place > 0).astype(F32)
    inside = jnp.where(row < 4, 1.0, jnp.where(row < 6, has_above, has_below))
    for at, tile, north, south in (
        (0, even, odd, pltpu.roll(odd, 1, 0)),
        (5, odd, pltpu.roll(even, 7, 0), even),
    ):
        shares = [
            0.5 * (tile + near)
            for near in (pltpu.roll(tile, width - 1, 1), pltpu.roll(tile, 1, 1), north, south)
        ]
        faces[at] = inside * (1.0 - ((shares[0] + shares[1]) + (shares[2] + shares[3])))
        for k, share in enumerate(shares):
            faces[at + 1 + k] = inside * share


def diffuse(faces, pair, u, h):
    width = u.shape[-1]

    def step(at, tile, north, south):
        lateral = faces[at + 1] * pltpu.roll(tile, width - 1, 1) + faces[at + 2] * pltpu.roll(tile, 1, 1)
        return (faces[at] * tile + lateral) + (faces[at + 3] * north + faces[at + 4] * south)

    put(pair, OWN, u)
    put(pair, BEYOND, h)
    even, odd = get(pair, EVEN), get(pair, ODD)
    for _ in range(STEPS):
        even, odd = step(0, even, odd, pltpu.roll(odd, 1, 0)), step(5, odd, pltpu.roll(even, 7, 0), even)
    put(pair, EVEN, even)
    put(pair, ODD, odd)
    return get(pair, OWN)


def place_of(index, bits):
    owner = 0
    for k, bit in enumerate(reversed(bits)):
        owner = owner + ((index >> k) & 1) * bit
    return owner


def index_of(owner, bits):
    index = 0
    for bit in bits:
        index = index * 2 + jnp.where((owner & bit) != 0, 1, 0)
    return index


def edges_kernel(width, alpha, kappa, perturb, *outs):
    members = alpha.shape[0]
    count = alpha.shape[1] // width
    even = lax.rem(lax.axis_index("space"), 2) == 0

    def send(chunk, at, rows):
        outs[2 * chunk][at] = jnp.where(even, rows[4:], rows[:4])
        outs[2 * chunk + 1][at] = jnp.where(even, rows[:4], rows[4:])

    def level(piece, carry):
        for chunk in range(width):
            for m in range(members):
                send(chunk, m * count + piece, alpha[m, piece * width + chunk])
        return carry

    lax.fori_loop(0, count, level, 0)
    send(0, members * count, kappa[...])


def forward_kernel(chunk, width, groups, alpha, beyond, k_beyond, kappa, land, perturb, *refs):
    faces, pair, outs = refs[-2], refs[-1], refs[:-2]
    members = perturb.shape[1]
    count = 2 * outs[0].shape[0]
    me = lax.axis_index("member")
    fill_faces(faces, pair.at[0], kappa[...], k_beyond[...])
    lead = groups[0][1]
    for half in (1, 0):
        def level(i, carry, half=half):
            owner = place_of(i, lead[1:]) + half * lead[0]
            piece = owner ^ me
            row = piece * width + chunk
            local = []
            for m in range(members):
                local.append(diffuse(faces, pair.at[m], alpha[m, row], beyond[m * count + piece]) * land[...].astype(F32))

            def added(t):
                total = perturb[t, 0, row].astype(F32) * local[0]
                for m in range(1, members):
                    total = total + perturb[t, m, row].astype(F32) * local[m]
                return total

            for g, (slots, order) in enumerate(groups):
                send, keep = outs[2 * g : 2 * g + 2]
                if order == lead:
                    for k, t in enumerate(slots):
                        (send if half else keep)[i, k] = added(t)
                else:
                    at = index_of(owner, order[1:])
                    sends = (owner & order[0]) != 0
                    values = [added(t) for t in slots]

                    @pl.when(sends)
                    def _(values=values, send=send, at=at):
                        for k, value in enumerate(values):
                            send[at, k] = value

                    @pl.when(jnp.logical_not(sends))
                    def _(values=values, keep=keep, at=at):
                        for k, value in enumerate(values):
                            keep[at, k] = value
            return carry

        lax.fori_loop(0, count // 2, level, 0)


def back_kernel(chunk, width, groups, perturb, land, *refs):
    back, to_partner, to_next = refs[-3:]
    given = refs[:-3]
    members = perturb.shape[1]
    count = 2 * given[0].shape[0]
    me = lax.axis_index("member")
    even = lax.rem(lax.axis_index("space"), 2) == 0
    lead = groups[0][1]
    for half in (0, 1):
        def level(i, carry, half=half):
            owner = place_of(i, lead[1:]) + half * lead[0]
            piece = owner ^ me
            row = piece * width + chunk
            sea = land[...].astype(F32)
            totals = [None] * members
            for g, (slots, order) in enumerate(groups):
                low, high = given[2 * g : 2 * g + 2]
                for k, t in enumerate(slots):
                    if order == lead:
                        value = (high if half else low)[i, k]
                    else:
                        at = index_of(owner, order[1:])
                        value = jnp.where((owner & order[0]) != 0, high[at, k], low[at, k])
                    for m in range(members):
                        term = perturb[t, m, row].astype(F32) * value
                        totals[m] = term if totals[m] is None else totals[m] + term
            for m in range(members):
                total = totals[m] * sea
                back[m, piece] = total
                to_partner[m * count + piece] = jnp.where(even, total[4:], total[:4])
                to_next[m * count + piece] = jnp.where(even, total[:4], total[4:])
            return carry

        lax.fori_loop(0, count // 2, level, 0)


def adjoint_kernel(chunk, width, alpha, back, beyond, k_beyond, kappa, *refs):
    gradient, faces, pair, stage, done = refs[-5:]
    members, count = back.shape[:2]
    fill_faces(faces, pair.at[0], kappa[...], k_beyond[...])

    def copy(m, piece):
        return pltpu.make_async_copy(
            stage.at[m, piece], gradient.at[m, piece * width + chunk], done.at[m, piece]
        )

    def level(piece, carry):
        for m in range(members):
            value = diffuse(faces, pair.at[m], back[m, piece], beyond[m * count + piece])
            stage[m, piece] = value + alpha[m, piece * width + chunk]
            copy(m, piece).start()
        return carry

    def finish(piece, carry):
        for m in range(members):
            copy(m, piece).wait()
        return carry

    lax.fori_loop(0, count, level, 0)
    lax.fori_loop(0, count, finish, 0)


VMEM = pl.BlockSpec(memory_space=pltpu.VMEM)
GRANT = pltpu.CompilerParams(vmem_limit_bytes=24 << 20)


def call(kernel, args, outs, scratch=()):
    return pl.pallas_call(
        kernel,
        out_shape=[jax.ShapeDtypeStruct(shape, F32) for shape in outs],
        in_specs=[VMEM] * len(args),
        out_specs=[VMEM] * len(outs),
        scratch_shapes=[pltpu.VMEM(shape, F32) for shape in scratch],
        compiler_params=GRANT,
    )(*args)


def exchange(x, bit):
    count = lax.axis_size("member")
    return lax.ppermute(x, "member", [(i, i ^ bit) for i in range(count)])


def to_partner_chip(x):
    ends = lax.axis_size("space")
    return lax.ppermute(x, "space", [(i, i ^ 1) for i in range(ends)])


def to_next_chip(x):
    ends = lax.axis_size("space")
    return lax.ppermute(x, "space", [(i, i + 1 if i % 2 else i - 1) for i in range(1, ends - 1)])


def halves(to_partner, to_next):
    near, far = to_partner_chip(to_partner), to_next_chip(to_next)
    even = lax.rem(lax.axis_index("space"), 2) == 0
    return jnp.concatenate([jnp.where(even, near, far), jnp.where(even, far, near)], axis=1)


def scatter(send, keep, bits):
    got = exchange(send, bits[0])
    for bit in bits[1:-1]:
        half = keep.shape[0] // 2
        send = keep[half:] + got[half:]
        keep = keep[:half] + got[:half]
        got = exchange(send, bit)
    return keep, got


def gather(held, bits):
    for k in range(len(bits) - 2, 0, -1):
        got = exchange(held, bits[k])
        held = jnp.concatenate([held, got], axis=0)
    return held, exchange(held, bits[0])


def inner(alpha, perturb, kappa, land, obs_weight, innovation):
    members, _, rows, lon = alpha.shape
    slots = perturb.shape[0]
    count = lax.axis_size("member")
    width = obs_weight.shape[1]
    bits = [1 << k for k in range(count.bit_length() - 1)]
    swapped = [bits[1], bits[0]] + bits[2:]
    early, late = tuple(range(slots // 2)), tuple(range(slots // 2, slots))
    plans = [((early, bits), (late, bits)) for _ in range(width - 1)]
    plans.append(((early, bits), (late, swapped)))

    shapes = [(members * count + (c == 0), 4, lon) for c in range(width) for _ in range(2)]
    edges = call(functools.partial(edges_kernel, width), (alpha, kappa, perturb), shapes)
    beyond = [halves(edges[2 * c], edges[2 * c + 1]) for c in range(width)]
    k_beyond = beyond[0][-1]

    far_weight = exchange(obs_weight, bits[-1])
    apart = {}
    for c in range(width):
        for g, (group, order) in enumerate(plans[c]):
            span = slice(group[0], group[-1] + 1)
            apart[c, g] = (innovation[span, c], jnp.stack([obs_weight[span, c], far_weight[span, c]]))
    apart = lax.optimization_barrier(apart)

    misfits = [[] for _ in range(width)]
    parts = [[] for _ in range(width)]
    for c in range(width):
        half = (count // 2,)
        shapes = [half + (len(group), rows, lon) for group, order in plans[c] for _ in range(2)]
        sums = call(
            functools.partial(forward_kernel, c, width, plans[c]),
            (alpha, beyond[c], k_beyond, kappa, land, perturb),
            shapes,
            [(10, rows, lon), (members, lon // LANES, 2 * rows, LANES)],
        )
        for g, (group, order) in enumerate(plans[c]):
            offset, weights = apart[c, g]
            keep, got = scatter(sums[2 * g], sums[2 * g + 1], order)
            both = keep + got
            both = jnp.stack([both[0] - offset, both[1]])
            got = exchange(both, bits[-1])
            misfit = weights * (both + got[::-1])
            misfits[c].append(misfit[0])
            parts[c].extend(gather(misfit, order))

    gradient = None
    for c in range(width):
        back, to_partner, to_next = call(
            functools.partial(back_kernel, c, width, plans[c]),
            (perturb, land, *parts[c]),
            [(members, count, rows, lon)] + [(members * count, 4, lon)] * 2,
        )
        args = [alpha, back, halves(to_partner, to_next), k_beyond, kappa]
        specs = [VMEM] * len(args)
        if gradient is not None:
            args.append(gradient)
            specs.append(pl.BlockSpec(memory_space=pl.ANY))
        gradient = pl.pallas_call(
            functools.partial(adjoint_kernel, c, width),
            out_shape=jax.ShapeDtypeStruct(alpha.shape, F32),
            in_specs=specs,
            out_specs=pl.BlockSpec(memory_space=pl.ANY),
            scratch_shapes=[
                pltpu.VMEM((10, rows, lon), F32),
                pltpu.VMEM((members, lon // LANES, 2 * rows, LANES), F32),
                pltpu.VMEM((members, count, rows, lon), F32),
                pltpu.SemaphoreType.DMA((members, count)),
            ],
            input_output_aliases={5: 0} if c else {},
            compiler_params=GRANT,
        )(*args)
    misfit = jnp.stack([jnp.concatenate(m, axis=0) for m in misfits], axis=1)
    return gradient, misfit


def solution(mesh):
    placed = (
        P("member", None, "space", None),
        P(None, "member", None, "space", None),
        P("space", None),
        P("space", None),
        P(None, "member", "space", None),
        P(None, "member", "space", None),
    )
    return jax.shard_map(
        inner,
        mesh=mesh,
        in_specs=placed,
        out_specs=(P("member", None, "space", None), P(None, "member", "space", None)),
        check_vma=False,
    )
```

```python
import functools

import jax
import jax.numpy as jnp
from jax import lax
from jax.experimental import pallas as pl
from jax.experimental.pallas import tpu as pltpu
from jax.sharding import PartitionSpec as P


STEPS = 4
F32 = jnp.float32


OWN, BEYOND = pl.ds(0, 8), pl.ds(8, 8)
EVEN, ODD = pl.ds(0, 8, stride=2), pl.ds(1, 8, stride=2)
LANES = 128


def put(pair, rows, value):
    for j in range(pair.shape[0]):
        pair[j, rows, :] = value[:, j * LANES : (j + 1) * LANES]


def get(pair, rows):
    return jnp.concatenate([pair[j, rows, :] for j in range(pair.shape[0])], axis=1)


def fill_faces(faces, pair, kappa, beyond):
    width = kappa.shape[-1]
    put(pair, OWN, kappa)
    put(pair, BEYOND, beyond)
    even, odd = get(pair, EVEN), get(pair, ODD)
    row = lax.broadcasted_iota(jnp.int32, kappa.shape, 0)
    place, count = lax.axis_index("space"), lax.axis_size("space")
    has_above = (place < count - 1).astype(F32)
    has_below = (place > 0).astype(F32)
    inside = jnp.where(row < 4, 1.0, jnp.where(row < 6, has_above, has_below))
    for at, tile, north, south in (
        (0, even, odd, pltpu.roll(odd, 1, 0)),
        (5, odd, pltpu.roll(even, 7, 0), even),
    ):
        shares = [
            0.5 * (tile + near)
            for near in (pltpu.roll(tile, width - 1, 1), pltpu.roll(tile, 1, 1), north, south)
        ]
        faces[at] = inside * (1.0 - ((shares[0] + shares[1]) + (shares[2] + shares[3])))
        for k, share in enumerate(shares):
            faces[at + 1 + k] = inside * share


def diffuse(faces, pair, u, h):
    width = u.shape[-1]

    def step(at, tile, north, south):
        lateral = faces[at + 1] * pltpu.roll(tile, width - 1, 1) + faces[at + 2] * pltpu.roll(tile, 1, 1)
        return (faces[at] * tile + lateral) + (faces[at + 3] * north + faces[at + 4] * south)

    put(pair, OWN, u)
    put(pair, BEYOND, h)
    even, odd = get(pair, EVEN), get(pair, ODD)
    for _ in range(STEPS):
        even, odd = step(0, even, odd, pltpu.roll(odd, 1, 0)), step(5, odd, pltpu.roll(even, 7, 0), even)
    put(pair, EVEN, even)
    put(pair, ODD, odd)
    return get(pair, OWN)


def place_of(index, bits):
    owner = 0
    for k, bit in enumerate(reversed(bits)):
        owner = owner + ((index >> k) & 1) * bit
    return owner


def index_of(owner, bits):
    index = 0
    for bit in bits:
        index = index * 2 + jnp.where((owner & bit) != 0, 1, 0)
    return index


def edges_kernel(width, alpha, kappa, *refs):
    held, cells, done = refs[-3:]
    outs = refs[:-3]
    members = alpha.shape[0]
    count = alpha.shape[1] // width
    even = lax.rem(lax.axis_index("space"), 2) == 0

    def copy(m):
        return pltpu.make_async_copy(alpha.at[m], held.at[m], done.at[m])

    def send(chunk, at, rows):
        outs[2 * chunk][at] = jnp.where(even, rows[4:], rows[:4])
        outs[2 * chunk + 1][at] = jnp.where(even, rows[:4], rows[4:])

    last = pltpu.make_async_copy(kappa, cells, done.at[members])
    for m in range(members):
        copy(m).start()
    last.start()
    for m in range(members):
        copy(m).wait()

        def level(piece, carry, m=m):
            for chunk in range(width):
                send(chunk, m * count + piece, held[m, piece * width + chunk])
            return carry

        lax.fori_loop(0, count, level, 0)
    last.wait()
    send(0, members * count, cells[...])


def forward_kernel(chunk, width, groups, parts, fetches, alpha, perturb, beyond, k_beyond, kappa, land, *refs):
    if fetches:
        fields, scales, got_field, got_scale = refs[-4:]
        refs = refs[:-4]
    faces, pair, outs = refs[-2], refs[-1], refs[:-2]
    _, members = perturb.shape[:2]
    count = alpha.shape[1] // width
    me = lax.axis_index("member")
    lead = groups[0][1]

    def owner_of(part, i):
        return place_of(i, lead[1:]) + parts[part] * lead[0]

    def copies(part, i):
        row = (owner_of(part, i) ^ me) * width + chunk
        at = part * (count // 2) + i
        return (
            pltpu.make_async_copy(alpha.at[:, row], fields.at[at], got_field.at[at]),
            pltpu.make_async_copy(perturb.at[:, :, row], scales.at[at], got_scale.at[at]),
        )

    for part in range(len(parts) if fetches else 0):
        def fetch(i, carry, part=part):
            for copy in copies(part, i):
                copy.start()
            return carry

        lax.fori_loop(0, count // 2, fetch, 0)
    fill_faces(faces, pair.at[0], kappa[...], k_beyond[...])
    for part, half in enumerate(parts):
        def level(i, carry, part=part, half=half):
            owner = owner_of(part, i)
            piece = owner ^ me
            row = piece * width + chunk
            if fetches:
                for copy in copies(part, i):
                    copy.wait()
                here = part * (count // 2) + i
                field = [fields[here, m] for m in range(members)]
                scale = lambda t, m: scales[here, t, m].astype(F32)
            else:
                field = [alpha[m, row] for m in range(members)]
                scale = lambda t, m: perturb[t, m, row].astype(F32)
            local = []
            for m in range(members):
                value = diffuse(faces, pair.at[m], field[m], beyond[m * count + piece])
                local.append(value * land[...].astype(F32))

            def added(t):
                total = scale(t, 0) * local[0]
                for m in range(1, members):
                    total = total + scale(t, m) * local[m]
                return total

            for g, (slots, order) in enumerate(groups):
                if len(parts) == 1:
                    out = outs[g]
                else:
                    send, keep = outs[2 * g : 2 * g + 2]
                    out = send if half else keep
                if order == lead:
                    for k, t in enumerate(slots):
                        out[i, k] = added(t)
                else:
                    at = index_of(owner, order[1:])
                    sends = (owner & order[0]) != 0
                    values = [added(t) for t in slots]

                    @pl.when(sends)
                    def _(values=values, send=send, at=at):
                        for k, value in enumerate(values):
                            send[at, k] = value

                    @pl.when(jnp.logical_not(sends))
                    def _(values=values, keep=keep, at=at):
                        for k, value in enumerate(values):
                            keep[at, k] = value
            return carry

        lax.fori_loop(0, count // 2, level, 0)


def back_kernel(chunk, width, groups, perturb, land, *refs):
    back, to_partner, to_next = refs[-3:]
    given = refs[:-3]
    members = perturb.shape[1]
    count = 2 * given[0].shape[0]
    me = lax.axis_index("member")
    even = lax.rem(lax.axis_index("space"), 2) == 0
    lead = groups[0][1]
    for half in (0, 1):
        def level(i, carry, half=half):
            owner = place_of(i, lead[1:]) + half * lead[0]
            piece = owner ^ me
            row = piece * width + chunk
            sea = land[...].astype(F32)
            totals = [None] * members
            for g, (slots, order) in enumerate(groups):
                low, high = given[2 * g : 2 * g + 2]
                for k, t in enumerate(slots):
                    if order == lead:
                        value = (high if half else low)[i, k]
                    else:
                        at = index_of(owner, order[1:])
                        value = jnp.where((owner & order[0]) != 0, high[at, k], low[at, k])
                    for m in range(members):
                        term = perturb[t, m, row].astype(F32) * value
                        totals[m] = term if totals[m] is None else totals[m] + term
            for m in range(members):
                total = totals[m] * sea
                back[m, piece] = total
                to_partner[m * count + piece] = jnp.where(even, total[4:], total[:4])
                to_next[m * count + piece] = jnp.where(even, total[:4], total[4:])
            return carry

        lax.fori_loop(0, count // 2, level, 0)


def adjoint_kernel(chunk, width, span, alpha, back, beyond, k_beyond, kappa, *refs):
    gradient, faces, pair, stage, done = refs[-5:]
    members, count = back.shape[:2]
    fill_faces(faces, pair.at[0], kappa[...], k_beyond[...])

    def copy(m, piece):
        at = piece - span[0]
        return pltpu.make_async_copy(
            stage.at[m, at], gradient.at[m, piece * width + chunk], done.at[m, at]
        )

    def level(piece, carry):
        for m in range(members):
            value = diffuse(faces, pair.at[m], back[m, piece], beyond[m * count + piece])
            stage[m, piece - span[0]] = value + alpha[m, piece * width + chunk]
            copy(m, piece).start()
        return carry

    def finish(piece, carry):
        for m in range(members):
            copy(m, piece).wait()
        return carry

    lax.fori_loop(*span, level, 0)
    lax.fori_loop(*span, finish, 0)


VMEM = pl.BlockSpec(memory_space=pltpu.VMEM)
GRANT = pltpu.CompilerParams(vmem_limit_bytes=8 << 20)


HERE = pl.BlockSpec(memory_space=pltpu.HBM)


def call(kernel, args, outs, scratch=(), left=0):
    args = [pltpu.with_memory_space_constraint(x, pltpu.HBM) if k < left else x for k, x in enumerate(args)]
    return pl.pallas_call(
        kernel,
        out_shape=[jax.ShapeDtypeStruct(shape, F32) for shape in outs],
        in_specs=[HERE] * left + [VMEM] * (len(args) - left),
        out_specs=[VMEM] * len(outs),
        scratch_shapes=list(scratch),
        compiler_params=GRANT,
    )(*args)


def exchange(x, bit):
    count = lax.axis_size("member")
    return lax.ppermute(x, "member", [(i, i ^ bit) for i in range(count)])


def to_partner_chip(x):
    ends = lax.axis_size("space")
    return lax.ppermute(x, "space", [(i, i ^ 1) for i in range(ends)])


def to_next_chip(x):
    ends = lax.axis_size("space")
    return lax.ppermute(x, "space", [(i, i + 1 if i % 2 else i - 1) for i in range(1, ends - 1)])


def halves(to_partner, to_next):
    near, far = to_partner_chip(to_partner), to_next_chip(to_next)
    even = lax.rem(lax.axis_index("space"), 2) == 0
    return jnp.concatenate([jnp.where(even, near, far), jnp.where(even, far, near)], axis=1)


def scatter(send, keep, bits):
    got = exchange(send, bits[0])
    for bit in bits[1:-1]:
        half = keep.shape[0] // 2
        send = keep[half:] + got[half:]
        keep = keep[:half] + got[:half]
        got = exchange(send, bit)
    return keep, got


def gather(held, bits):
    for k in range(len(bits) - 2, 0, -1):
        got = exchange(held, bits[k])
        held = jnp.concatenate([held, got], axis=0)
    return held, exchange(held, bits[0])


def inner(alpha, perturb, kappa, land, obs_weight, innovation):
    members, _, rows, lon = alpha.shape
    slots = perturb.shape[0]
    count = lax.axis_size("member")
    width = obs_weight.shape[1]
    bits = [1 << k for k in range(count.bit_length() - 1)]
    swapped = [bits[1], bits[0]] + bits[2:]
    early, late = tuple(range(slots // 2)), tuple(range(slots // 2, slots))
    plans = [((early, bits), (late, bits)) for _ in range(width - 1)]
    plans.append(((early, bits), (late, swapped)))

    shapes = [(members * count + (c == 0), 4, lon) for c in range(width) for _ in range(2)]
    edges = call(
        functools.partial(edges_kernel, width),
        (alpha, kappa),
        shapes,
        [
            pltpu.VMEM(alpha.shape, F32),
            pltpu.VMEM(kappa.shape, F32),
            pltpu.SemaphoreType.DMA((members + 1,)),
        ],
        left=2,
    )
    beyond = [halves(edges[2 * c], edges[2 * c + 1]) for c in range(width)]
    k_beyond = beyond[0][-1]

    far_weight = exchange(obs_weight, bits[-1])
    apart = {}
    for c in range(width):
        for g, (group, order) in enumerate(plans[c]):
            span = slice(group[0], group[-1] + 1)
            apart[c, g] = (innovation[span, c], jnp.stack([obs_weight[span, c], far_weight[span, c]]))
    apart = lax.optimization_barrier(apart)

    misfits = [[] for _ in range(width)]
    parts = [[] for _ in range(width)]
    for c in range(width):
        half = count // 2
        whole = any(order != bits for group, order in plans[c])
        sums = [[], []]
        for name, parts_of in (("", (1, 0)),) if whole else (("a", (1,)), ("b", (0,))):
            room = half * len(parts_of)
            scratch = [
                pltpu.VMEM((10, rows, lon), F32),
                pltpu.VMEM((members, lon // LANES, 2 * rows, LANES), F32),
            ]
            fetches = name == "a"
            if fetches:
                scratch += [
                    pltpu.VMEM((room, members, rows, lon), F32),
                    pltpu.VMEM((room, slots, members, rows, lon), perturb.dtype),
                    pltpu.SemaphoreType.DMA((room,)),
                    pltpu.SemaphoreType.DMA((room,)),
                ]
            made = call(
                functools.partial(forward_kernel, c, width, plans[c], parts_of, fetches),
                (alpha, perturb, beyond[c], k_beyond, kappa, land),
                [(half, len(group), rows, lon) for group, order in plans[c] for k in parts_of],
                scratch,
                left=2 * fetches,
            )
            for k, part in enumerate(parts_of):
                sums[1 - part].extend(made[k :: len(parts_of)])
        for g, (group, order) in enumerate(plans[c]):
            name = f"c{c}g{g}"
            offset, weights = apart[c, g]
            keep, got = scatter(sums[0][g], sums[1][g], order)
            both = keep + got
            both = jnp.stack([both[0] - offset, both[1]])
            got = exchange(both, bits[-1])
            misfit = weights * (both + got[::-1])
            misfits[c].append(misfit[0])
            parts[c].extend(gather(misfit, order))

    gradient = None
    for c in range(width):
        back, to_partner, to_next = call(
            functools.partial(back_kernel, c, width, plans[c]),
            (perturb, land, *parts[c]),
            [(members, count, rows, lon)] + [(members * count, 4, lon)] * 2,
        )
        spans = ((0, count),)
        around = halves(to_partner, to_next)
        for span in spans:
            args = [alpha, back, around, k_beyond, kappa]
            specs = [VMEM] * len(args)
            if gradient is not None:
                args.append(gradient)
                specs.append(HERE)
            gradient = pl.pallas_call(
                functools.partial(adjoint_kernel, c, width, span),
                out_shape=jax.ShapeDtypeStruct(alpha.shape, F32),
                in_specs=specs,
                out_specs=HERE,
                scratch_shapes=[
                    pltpu.VMEM((10, rows, lon), F32),
                    pltpu.VMEM((members, lon // LANES, 2 * rows, LANES), F32),
                    pltpu.VMEM((members, span[1] - span[0], rows, lon), F32),
                    pltpu.SemaphoreType.DMA((members, span[1] - span[0])),
                ],
                input_output_aliases={5: 0} if len(args) > 5 else {},
                compiler_params=GRANT,
            )(*args)
    misfit = jnp.stack([jnp.concatenate(m, axis=0) for m in misfits], axis=1)
    return gradient, misfit


def solution(mesh):
    placed = (
        P("member", None, "space", None),
        P(None, "member", None, "space", None),
        P("space", None),
        P("space", None),
        P(None, "member", "space", None),
        P(None, "member", "space", None),
    )
    return jax.shard_map(
        inner,
        mesh=mesh,
        in_specs=placed,
        out_specs=(P("member", None, "space", None), P(None, "member", "space", None)),
        check_vma=False,
    )
```
